32 devices in a mesh: clips: 2 (over x), seq: 16 (over z, y, core).
Axes of the slice: x: 2, y: 2, z: 4, core: 2. Of those that a mesh axis runs over, the one named last changes fastest.
Arguments:
- video_q: bfloat16 [4096, 1536], P(('clips', 'seq')), parts along dimension 0, may hold values from -200 to 200
- video_k: bfloat16 [4096, 1536], P(('clips', 'seq')), parts along dimension 0, may hold values from -7 to 7
- video_v: bfloat16 [4096, 1536], P(('clips', 'seq')), parts along dimension 0, may hold values from -6 to 6
- audio_q: bfloat16 [256, 1536], P(('clips', 'seq')), parts along dimension 0, may hold values from -200 to 200
- audio_k: bfloat16 [256, 1536], P(('clips', 'seq')), parts along dimension 0, may hold values from -6 to 6
- audio_v: bfloat16 [256, 1536], P(('clips', 'seq')), parts along dimension 0, may hold values from -6 to 6
- radius: int32 [32], P(('clips', 'seq')), parts along dimension 0, may hold values from 1 to 2
- tile_list: int32 [32, 5], P('clips'), parts along dimension 0, may hold values from -1 to 15, as said below
- tile_count: int32 [32], P('clips'), parts along dimension 0, may hold values from 1 to 5, as said below
- video_gain: float32 [1536], replicated, may hold values from 0.5 to 1.5
- audio_gain: float32 [1536], replicated, may hold values from 0.5 to 1.5
Outputs:
- video_out: bfloat16 [4096, 1536], P(('clips', 'seq')), parts along dimension 0
- audio_out: bfloat16 [256, 1536], P(('clips', 'seq')), parts along dimension 0
The draws below stay inside these ranges and needn't reach their ends.
There are 2 independent parts, one for each index of `clips`. The reference program is written for one: setup_inputs(seed, part) draws one part's arguments, and reference() takes and returns one part's arrays. A program takes and returns all parts, laid end to end along the dimension named above; an argument that names none is the same for every part. Nothing has to cross between parts.
Inputs may be any that keep to these rules, and one draw needn't show every extreme that they name: `tile_list`: row b names tile b first, then tile_count[b] - 1 distinct other tiles within 4 of b; the remaining entries are -1. `tile_count`: some block lists 5 tiles.
All inputs are finite; a program needn't handle non-finite values.
Results may differ from the reference program's by a relative error of at most 0.014.
Values may be sent and summed in bfloat16 or wider, within the bound.
No kernel may reach another device: no remote copies, remote signals or barrier semaphores. Data moves between devices by JAX's collectives and lax.ppermute only.
A program may use at most 64 MiB of HBM per device.

```python
import jax
import jax.numpy as jnp
from jax import lax

H = 12
HD = 128
D = 1536
TOK_DEV = 128
AUD_DEV = 8
RMAX = 2
SPAN = 4
LMAX = 5
TILES = 16
NV = 2048
NA = 128


def key_field(key):
    drawn = jnp.clip(jax.random.normal(jax.random.fold_in(key, 101), (NV, D), jnp.float32), -6.0, 6.0)
    return drawn


def draw_video_k(key, part):
    return key_field(key).astype(jnp.bfloat16)


def draw_video_q(key, part):
    drawn = jnp.clip(jax.random.normal(jax.random.fold_in(key, 103), (NV, D), jnp.float32), -6.0, 6.0)
    return drawn.astype(jnp.bfloat16)


def draw_audio_q(key, part):
    drawn = jnp.clip(jax.random.normal(jax.random.fold_in(key, 106), (NA, D), jnp.float32), -6.0, 6.0)
    return drawn.astype(jnp.bfloat16)


def tile_tables(key):
    base_key = jax.random.fold_in(key, 201)
    block_counts = jax.random.randint(jax.random.fold_in(base_key, 1), (TILES,), 1, LMAX + 1)
    full_block = jax.random.randint(jax.random.fold_in(base_key, 2), (), 0, TILES)
    block_counts = jnp.where(jnp.arange(TILES) == full_block, LMAX, block_counts).astype(jnp.int32)
    candidate_offsets = jnp.concatenate([jnp.arange(-SPAN, 0), jnp.arange(1, SPAN + 1)])
    blocks = jnp.arange(TILES)[:, None]
    candidate = blocks + candidate_offsets[None, :]
    usable = (candidate >= 0) & (candidate < TILES)
    width_index = jnp.arange(2 * SPAN)[None, :]
    random_score = jax.random.randint(jax.random.fold_in(base_key, 3), (TILES, 2 * SPAN), 0, 1024) * 64 + width_index
    rank_score = jnp.where(usable, random_score, (1 << 20) + width_index)
    ordering = jnp.argsort(rank_score, axis=1, stable=True)
    picked = jnp.take_along_axis(candidate, ordering[:, :LMAX - 1], axis=1)
    tile_rows = jnp.concatenate([blocks, picked], axis=1)
    tile_rows = jnp.where(jnp.arange(LMAX)[None, :] < block_counts[:, None], tile_rows, -1)
    return (tile_rows.astype(jnp.int32), block_counts)


def draw_tile_list(key, part):
    return tile_tables(key)[0]


def draw_tile_count(key, part):
    return tile_tables(key)[1]


def place_ends(values, rng, smallest, high):
    dims = values.shape
    place = [jax.random.randint(jax.random.fold_in(rng, axis), (), 0, dims[axis]) for axis in range(len(dims))]
    values = values.at[tuple(place)].set(smallest)
    longest = dims.index(max(dims))
    place[longest] = (place[longest] + 1) % dims[longest]
    return values.at[tuple(place)].set(high)


def levels(rng, extent, split, least, high):
    loudness = 1.0
    for axis_at, shards_of in split:
        steps = jax.random.uniform(jax.random.fold_in(jax.random.fold_in(rng, 6), axis_at), (shards_of,), jnp.float32, least / len(split), high / len(split))
        loudness = loudness * jnp.repeat(jnp.exp(steps), extent[axis_at] // shards_of).reshape((-1,) + (1,) * (len(extent) - 1 - axis_at))
    return loudness


def centred(rng, extent, deviation, most, cuts=(), held_as=jnp.bfloat16):
    values = jax.random.normal(rng, extent, jnp.float32) * deviation
    if len(cuts) > 0:
        values = levels(rng, extent, cuts, -0.22, 0.18) * values
    return jnp.clip(values, min=-most, max=most).astype(held_as)


def setup_inputs(seed: int = 0, part: int = 0) -> dict:
    arg_keys = jax.random.split(jax.random.key(seed), 12)
    part_keys = jax.random.split(jax.random.fold_in(arg_keys[11], part), 12)
    video_q = draw_video_q(jax.random.fold_in(jax.random.fold_in(arg_keys[11], part), 71), part)
    video_k = draw_video_k(jax.random.fold_in(jax.random.fold_in(arg_keys[11], part), 71), part)
    video_v = centred(part_keys[2], (NV, D), 1.0, 6.0, ((0, 16),))
    audio_q = draw_audio_q(jax.random.fold_in(jax.random.fold_in(arg_keys[11], part), 71), part)
    audio_k = centred(part_keys[4], (NA, D), 1.0, 6.0, ((0, 16),))
    audio_v = centred(part_keys[5], (NA, D), 1.0, 6.0, ((0, 16),))
    radius = place_ends(jax.random.randint(part_keys[6], (TILES,), 1, RMAX + 1), jax.random.fold_in(part_keys[6], 1), 1, RMAX).astype(jnp.int32)
    tile_list = draw_tile_list(jax.random.fold_in(jax.random.fold_in(arg_keys[11], part), 71), part)
    tile_count = draw_tile_count(jax.random.fold_in(jax.random.fold_in(arg_keys[11], part), 71), part)
    video_gain = jnp.clip(1.0 + 0.1 * jax.random.normal(arg_keys[9], (D,), jnp.float32), 0.5, 1.5)
    audio_gain = jnp.clip(1.0 + 0.1 * jax.random.normal(arg_keys[10], (D,), jnp.float32), 0.5, 1.5)
    return dict(video_q=video_q, video_k=video_k, video_v=video_v, audio_q=audio_q, audio_k=audio_k, audio_v=audio_v, radius=radius, tile_list=tile_list, tile_count=tile_count, video_gain=video_gain, audio_gain=audio_gain)


negative_big = -1e+30
epsilon = 1e-06

def split_heads(matrix):
    return matrix.astype(jnp.float32).reshape(matrix.shape[0], H, HD)

def softmax_attend(queries, key_rows, value_rows, key_valid):
    scores = jnp.einsum('qhd,khd->hqk', split_heads(queries), split_heads(key_rows)) * HD ** (-0.5)
    scores = jnp.where(key_valid[None, None, :], scores, negative_big)
    row_peak = lax.optimization_barrier(jnp.max(scores, axis=-1, keepdims=True))
    weights = jnp.exp(scores - row_peak).astype(jnp.bfloat16)
    weights = lax.optimization_barrier(weights).astype(jnp.float32)
    weight_sum = lax.optimization_barrier(jnp.sum(weights, axis=-1))
    mixed = jnp.einsum('hqk,khd->hqd', weights, split_heads(value_rows)) / weight_sum[..., None]
    return jnp.transpose(mixed, (1, 0, 2)).reshape(queries.shape[0], H * HD)

def rms_scale(mixed, gain):
    mean_square = lax.optimization_barrier(jnp.mean(mixed * mixed, axis=-1, keepdims=True))
    return (mixed * lax.rsqrt(mean_square + epsilon) * gain.astype(jnp.float32)).astype(jnp.bfloat16)

def reference(video_q, video_k, video_v, audio_q, audio_k, audio_v, radius, tile_list, tile_count, video_gain, audio_gain):
    span_tiles = 2 * RMAX + 1
    key_tiles = jnp.pad(video_k.reshape(TILES, TOK_DEV, D), ((RMAX, RMAX), (0, 0), (0, 0)))
    value_tiles = jnp.pad(video_v.reshape(TILES, TOK_DEV, D), ((RMAX, RMAX), (0, 0), (0, 0)))
    query_tiles = video_q.reshape(TILES, TOK_DEV, D)
    offsets = jnp.arange(-RMAX, RMAX + 1, dtype=jnp.int32)

    def video_tile(tile_index):
        start = (tile_index, jnp.int32(0), jnp.int32(0))
        window_keys = lax.dynamic_slice(key_tiles, start, (span_tiles, TOK_DEV, D)).reshape(span_tiles * TOK_DEV, D)
        window_values = lax.dynamic_slice(value_tiles, start, (span_tiles, TOK_DEV, D)).reshape(span_tiles * TOK_DEV, D)
        neighbour = tile_index + offsets
        tile_valid = (jnp.abs(offsets) <= radius[tile_index]) & (neighbour >= 0) & (neighbour < TILES)
        key_valid = jnp.concatenate([jnp.repeat(tile_valid, TOK_DEV), jnp.ones((NA,), dtype=bool)])
        key_rows = jnp.concatenate([window_keys, audio_k], axis=0)
        value_rows = jnp.concatenate([window_values, audio_v], axis=0)
        queries = lax.dynamic_index_in_dim(query_tiles, tile_index, 0, keepdims=False)
        return softmax_attend(queries, key_rows, value_rows, key_valid)
    video_mixed = lax.map(video_tile, jnp.arange(TILES, dtype=jnp.int32))
    video_out = rms_scale(video_mixed.reshape(NV, D), video_gain)
    audio_tiles = audio_q.reshape(TILES, AUD_DEV, D)
    video_key_tiles = video_k.reshape(TILES, TOK_DEV, D)
    video_value_tiles = video_v.reshape(TILES, TOK_DEV, D)

    def audio_block(block_index):
        listed = tile_list[block_index]
        chosen = jnp.maximum(listed, 0).astype(jnp.int32)
        key_rows = video_key_tiles[chosen].reshape(LMAX * TOK_DEV, D)
        value_rows = video_value_tiles[chosen].reshape(LMAX * TOK_DEV, D)
        entry_valid = jnp.arange(LMAX, dtype=jnp.int32) < tile_count[block_index]
        key_valid = jnp.repeat(entry_valid, TOK_DEV)
        queries = lax.dynamic_index_in_dim(audio_tiles, block_index, 0, keepdims=False)
        return softmax_attend(queries, key_rows, value_rows, key_valid)
    audio_mixed = lax.map(audio_block, jnp.arange(TILES, dtype=jnp.int32))
    audio_out = rms_scale(audio_mixed.reshape(NA, D), audio_gain)
    return (video_out, audio_out)
```

```python
import functools
import math

import jax
import jax.numpy as jnp
from jax import lax
from jax.experimental import pallas as pl
from jax.experimental.pallas import tpu as pltpu
from jax.sharding import PartitionSpec as P

H = 12
HD = 128
RMAX = 2
SPAN = 4

GROUP = SPAN
SHARE = H // GROUP
COLS = SHARE * HD

NEG = -1e30
EPS = 1e-06
SCALE = math.log2(math.e) / math.sqrt(HD)


VMEM_GRANT = 16 * 1024 * 1024

VM = pl.BlockSpec(memory_space=pltpu.VMEM)
SM = pl.BlockSpec(memory_space=pltpu.SMEM)
f32 = jnp.float32
bf16 = jnp.bfloat16


def call(body, outs, ins, name, flops=0, smem=0):
    total = sum(math.prod(o.shape) * o.dtype.itemsize for o in outs)
    total += sum(math.prod(i.shape) * i.dtype.itemsize for i in ins)
    return pl.pallas_call(
        body,
        out_shape=list(outs),
        in_specs=[SM] * smem + [VM] * (len(ins) - smem),
        out_specs=[VM] * len(outs),
        name=name,
        compiler_params=pltpu.CompilerParams(vmem_limit_bytes=VMEM_GRANT),
        cost_estimate=pl.CostEstimate(flops=flops, bytes_accessed=total, transcendentals=0),
    )(*ins)


def sds(rows, cols, dtype=bf16):
    return jax.ShapeDtypeStruct((rows, cols), dtype)


def share_cols(step):
    share = lax.rem(lax.axis_index("seq"), GROUP) ^ step
    return pl.ds(pl.multiple_of(share * COLS, HD), COLS)


def stack_rows(first, second):
    return jnp.concatenate([first.astype(f32), second.astype(f32)], axis=0).astype(bf16)


def audio_pair(radius, aq, ak, av, cols):
    rad = jnp.full((aq.shape[0], COLS), radius[0].astype(f32), f32)
    return stack_rows(aq[:, cols], ak[:, cols]), stack_rows(av[:, cols], rad)


def pack_keys(rows, aud, radius, k, aq, ak, av, ka2, ka3):
    for step, out in ((2, ka2), (3, ka3)):
        cols = share_cols(step)
        out[:rows] = k[:, cols]
        first, second = audio_pair(radius, aq, ak, av, cols)
        out[rows : rows + 2 * aud] = first
        out[rows + 2 * aud :] = second


def pack_rest(rows, aud, radius, q, k, v, aq, ak, av, v2, v3, q2, q3, kv1, qa1, kv0, qa0):
    for step, vo, qo in ((2, v2, q2), (3, v3, q3)):
        cols = share_cols(step)
        vo[...] = v[:, cols]
        qo[...] = q[:, cols]
    for step, kvo, qao in ((1, kv1, qa1), (0, kv0, qa0)):
        cols = share_cols(step)
        kvo[:rows] = k[:, cols]
        kvo[rows:] = v[:, cols]
        qao[:rows] = q[:, cols]
        first, second = audio_pair(radius, aq, ak, av, cols)
        qao[rows : rows + 2 * aud] = first
        qao[rows + 2 * aud :] = second


def relay(rows, aud, qa0, qa1, ka2, ka3, az, hk):
    hk[:rows] = ka2[:rows]
    hk[rows:] = ka3[:rows]
    parts = [ref[rows : rows + 3 * aud].astype(f32) for ref in (qa0, qa1, ka2, ka3)]
    for which in range(3):
        stacked = [part[which * aud : (which + 1) * aud] for part in parts]
        az[which * GROUP * aud : (which + 1) * GROUP * aud] = jnp.concatenate(stacked, 0).astype(bf16)


def head(value, index):
    return value[:, index * HD : (index + 1) * HD]


def scores_of(queries, keys):
    return lax.dot_general(queries, keys, (((1,), (1,)), ((), ())), preferred_element_type=f32)


def softmax_part(scores, values):
    peak = jnp.max(scores, axis=-1, keepdims=True)
    weights = jnp.exp2((scores - peak) * SCALE).astype(bf16)
    total = jnp.sum(weights.astype(f32), axis=-1, keepdims=True)
    mixed = jnp.dot(weights, values, preferred_element_type=f32)
    return peak, total, mixed


def in_lanes(columns):
    rows = columns[0].shape[0]
    lane = lax.broadcasted_iota(jnp.int32, (rows, HD), 1)
    out = jnp.zeros((rows, HD), f32)
    for index, column in enumerate(columns):
        out = jnp.where(lane == index, column, out)
    return out


def window_bias(radius_row, query_tile, key_tile, tiles):
    inside = (key_tile >= 0) & (key_tile < tiles)
    distance = jnp.where(inside, jnp.abs(query_tile - key_tile), tiles).astype(f32)
    return jnp.where(radius_row >= distance, 0.0, NEG).astype(f32)


def audio_partial(
    rows, aud, tiles, tile_list, tile_count, kv0, kv1, ka2, v2, ka3, v3, az, az_prev, az_next, p_prev, p_own, p_next
):
    me = lax.axis_index("seq")
    span = GROUP * aud
    lists = tile_list.shape[1]
    sources = ((me, az), (lax.rem(me + tiles - GROUP, tiles), az_prev), (lax.rem(me + GROUP, tiles), az_next))
    bias_rows = []
    for base, _ in sources:
        for member in range(GROUP):
            block = base ^ member
            hits = [jnp.int32(0)] * GROUP
            count = tile_count[block]
            for entry in range(lists):
                listed = jnp.where(entry < count, tile_list[block, entry], -1)
                for step in range(GROUP):
                    hits[step] = jnp.where(listed == (me ^ step), 1, hits[step])
            bias_rows.append(
                jnp.concatenate(
                    [jnp.full((aud, rows), jnp.where(hit > 0, 0.0, NEG).astype(f32), f32) for hit in hits], axis=1
                )
            )
    bias = jnp.concatenate(bias_rows, axis=0)
    results = []
    for index in range(SHARE):
        here = slice(index * HD, (index + 1) * HD)
        queries = jnp.concatenate([ref[:span, here] for _, ref in sources], axis=0)
        keys = jnp.concatenate([kv0[:rows, here], kv1[:rows, here], ka2[:rows, here], ka3[:rows, here]], axis=0)
        values = jnp.concatenate([kv0[rows:, here], kv1[rows:, here], v2[:, here], v3[:, here]], axis=0)
        results.append(softmax_part(scores_of(queries, keys) + bias, values))
    marks = in_lanes([r[0] for r in results] + [r[1] for r in results])
    for which, out in enumerate((p_own, p_prev, p_next)):
        part = slice(which * span, (which + 1) * span)
        for index in range(SHARE):
            out[:, index * HD : (index + 1) * HD] = results[index][2][part]
        out[:, COLS:] = marks[part]


def audio_keys_of(span, az, others, here):
    keys, values = [az[span : 2 * span, here]], [az[2 * span : 3 * span, here]]
    for ref in others:
        start = ref.shape[0] - 2 * span
        keys.append(ref[start : start + span, here])
        values.append(ref[start + span : start + 2 * span, here])
    return keys, values


def near_part(rows, aud, tiles, qa0, qa1, kv0, kv1, ka2, v2, ka3, v3, az, *rest):
    others, (acc, marks) = rest[:-2], rest[-2:]
    me = lax.axis_index("seq")
    span = GROUP * aud
    peaks, totals = {}, {}
    for which, qa in enumerate((qa0, qa1)):
        radius_row = qa[rows + 2 * aud :, :HD].astype(f32)[aud : aud + 1]
        biases = [window_bias(radius_row, me ^ which, me ^ step, tiles) for step in range(GROUP)]
        columns = []
        for index in range(SHARE):
            here = slice(index * HD, (index + 1) * HD)
            ak, av = audio_keys_of(span, az, others, here)
            keys = jnp.concatenate([kv0[:rows, here], kv1[:rows, here], ka2[:rows, here], ka3[:rows, here]] + ak, 0)
            values = jnp.concatenate([kv0[rows:, here], kv1[rows:, here], v2[:, here], v3[:, here]] + av, 0)
            audio_count = keys.shape[0] - GROUP * rows
            bias = jnp.concatenate(biases + [jnp.zeros((1, audio_count), f32)], axis=1)
            peak, total, mixed = softmax_part(scores_of(qa[:rows, here], keys) + bias, values)
            acc[which * rows : (which + 1) * rows, here] = mixed
            columns.append((peak, total))
        marks[which * rows : (which + 1) * rows] = in_lanes([c[0] for c in columns] + [c[1] for c in columns])


def halo_tile(me, tiles, which):
    low_half = lax.rem(me, GROUP) < GROUP // 2
    ahead = low_half if which == 0 else jnp.logical_not(low_half)
    return jnp.where(ahead, me + GROUP, me - GROUP)


def far_part(
    rows, aud, tiles, q2, q3, kv0, kv1, ka2, v2, ka3, v3, h0, h1, p_own, r_prev, r_next, az, *rest
):
    others, (o2, o3, ao) = rest[:-3], rest[-3:]
    me = lax.axis_index("seq")
    span = GROUP * aud
    zone = me // GROUP
    first = halo_tile(me, tiles, 0)
    key_tiles = [me, me ^ 1, me ^ 2, me ^ 3, first, first ^ 1]
    for which, query, ka, out in ((2, q2, ka2, o2), (3, q3, ka3, o3)):
        radius_row = ka[rows + 2 * aud :, :HD].astype(f32)[aud : aud + 1]
        biases = [window_bias(radius_row, me ^ which, tile, tiles) for tile in key_tiles]
        for index in range(SHARE):
            here = slice(index * HD, (index + 1) * HD)
            ak, av = audio_keys_of(span, az, others, here)
            keys = jnp.concatenate(
                [kv0[:rows, here], kv1[:rows, here], ka2[:rows, here], ka3[:rows, here], h0[:rows, here], h1[:rows, here]]
                + ak,
                0,
            )
            values = jnp.concatenate(
                [kv0[rows:, here], kv1[rows:, here], v2[:, here], v3[:, here], h0[rows:, here], h1[rows:, here]] + av, 0
            )
            audio_count = keys.shape[0] - len(key_tiles) * rows
            bias = jnp.concatenate(biases + [jnp.zeros((1, audio_count), f32)], axis=1)
            _, total, mixed = softmax_part(scores_of(query[:, here], keys) + bias, values)
            out[:rows, here] = (mixed / total).astype(bf16)
    for index in range(SHARE):
        here = slice(index * HD, (index + 1) * HD)
        parts = []
        for ref, there in ((p_own, None), (r_prev, zone > 0), (r_next, zone < tiles // GROUP - 1)):
            peak = ref[:, COLS + index : COLS + index + 1]
            if there is not None:
                peak = jnp.where(there, peak, NEG)
            parts.append((peak, ref[:, COLS + SHARE + index : COLS + SHARE + index + 1], ref[:, here]))
        top = functools.reduce(jnp.maximum, [part[0] for part in parts])
        total, mixed = 0.0, 0.0
        for peak, part_total, part_mixed in parts:
            shrink = jnp.exp2((peak - top) * SCALE)
            total = total + part_total * shrink
            mixed = mixed + part_mixed * shrink
        done = mixed / total
        zeros = jnp.zeros((aud, HD), f32)
        ao[:, here] = done[: 2 * aud].astype(bf16)
        o2[rows:, here] = jnp.concatenate([done[2 * aud : 3 * aud], zeros], 0).astype(bf16)
        o3[rows:, here] = jnp.concatenate([done[3 * aud :], zeros], 0).astype(bf16)


def last_part(rows, aud, tiles, qa0, qa1, acc, marks, hk, hv2, hv3, ao, o0, o1):
    me = lax.axis_index("seq")
    base = halo_tile(me, tiles, 1)
    key_tiles = [base ^ 2, base ^ 3]
    for which, qa, out in ((0, qa0, o0), (1, qa1, o1)):
        radius_row = qa[rows + 2 * aud :, :HD].astype(f32)[aud : aud + 1]
        bias = jnp.concatenate([window_bias(radius_row, me ^ which, tile, tiles) for tile in key_tiles], axis=1)
        band = slice(which * rows, (which + 1) * rows)
        for index in range(SHARE):
            here = slice(index * HD, (index + 1) * HD)
            values = jnp.concatenate([hv2[:, here], hv3[:, here]], axis=0)
            scores = scores_of(qa[:rows, here], hk[:, here]) + bias
            old_peak = marks[band, index : index + 1]
            old_total = marks[band, SHARE + index : SHARE + index + 1]
            peak = jnp.maximum(old_peak, jnp.max(scores, axis=-1, keepdims=True))
            shrink = jnp.exp2((old_peak - peak) * SCALE)
            weights = jnp.exp2((scores - peak) * SCALE).astype(bf16)
            total = old_total * shrink + jnp.sum(weights.astype(f32), axis=-1, keepdims=True)
            mixed = acc[band, here] * shrink + jnp.dot(weights, values, preferred_element_type=f32)
            out[:rows, here] = (mixed / total).astype(bf16)
        audio = ao[...].astype(f32)
        zeros = jnp.zeros((aud, COLS), f32)
        out[rows:] = jnp.concatenate([audio[which * aud : (which + 1) * aud], zeros], 0).astype(bf16)


def normalize(rows, aud, gain_v, gain_a, o0, o1, o2, o3, video, audio):
    parts = [ref[...].astype(f32) for ref in (o0, o1, o2, o3)]
    square = sum(jnp.sum(part * part, axis=-1, keepdims=True) for part in parts)
    factor = lax.rsqrt(square / (H * HD) + EPS)
    for step, part in enumerate(parts):
        cols = share_cols(step)
        scaled = part * factor
        video[:, cols] = (scaled[:rows] * gain_v[:, cols]).astype(bf16)
        audio[:, cols] = (scaled[rows : rows + aud] * gain_a[:, cols]).astype(bf16)


def on_device(
    video_q,
    video_k,
    video_v,
    audio_q,
    audio_k,
    audio_v,
    radius,
    tile_list,
    tile_count,
    video_gain,
    audio_gain,
):
    tiles = lax.axis_size("seq")
    groups = tiles // GROUP
    rows, aud = video_q.shape[0], audio_q.shape[0]
    span = GROUP * aud
    padded = rows + 2 * aud
    payload = rows + 4 * aud

    def swap(value, step):
        return lax.ppermute(value, "seq", [(i, i ^ step) for i in range(tiles)])

    def shift(value, steps):
        pairs = [(i, i + steps) for i in range(tiles) if 0 <= i + steps < tiles]
        return lax.ppermute(value, "seq", pairs)

    def turn(value, zones):
        return lax.ppermute(value, "seq", [(i, (i + zones * GROUP) % tiles) for i in range(tiles)])

    def outward(value, flip):
        pairs = []
        for i in range(tiles):
            low_half = i % GROUP < GROUP // 2
            to = i + GROUP if low_half == flip else i - GROUP
            if 0 <= to < tiles:
                pairs.append((i, to))
        return lax.ppermute(value, "seq", pairs)

    size = dict(rows=rows, aud=aud)
    dims = (rows, aud, tiles)
    my_k, my_rest = (radius, video_k, audio_q, audio_k, audio_v), (
        radius,
        video_q,
        video_k,
        video_v,
        audio_q,
        audio_k,
        audio_v,
    )
    ka2, ka3 = call(functools.partial(pack_keys, rows, aud), [sds(payload, COLS)] * 2, my_k, "pack_keys", smem=1)
    ka2, ka3 = swap(ka2, 2), swap(ka3, 3)
    v2, v3, q2, q3, kv1, qa1, kv0, qa0 = call(
        functools.partial(pack_rest, rows, aud),
        [sds(rows, COLS)] * 4 + [sds(2 * rows, COLS), sds(payload, COLS)] * 2,
        my_rest,
        "pack_rest",
        smem=1,
    )
    v2, v3 = swap(v2, 2), swap(v3, 3)
    q2, q3 = swap(q2, 2), swap(q3, 3)
    kv1, qa1 = swap(kv1, 1), swap(qa1, 1)
    h0 = outward(kv0, False)
    h1 = outward(kv1, False)
    az, hk = call(
        functools.partial(relay, rows, aud),
        [sds(3 * span, COLS), sds(2 * rows, COLS)],
        (qa0, qa1, ka2, ka3),
        "relay",
    )
    rounds = {}
    for zone in range(1, groups):
        near = zone in (1, groups - 1)
        rounds[zone] = turn(az if near else az[span:], zone)
    hk = outward(hk, True)
    hv2, hv3 = outward(v2, True), outward(v3, True)
    others = [rounds[zone] for zone in sorted(rounds)]

    group_keys = (kv0, kv1, ka2, v2, ka3, v3)
    p_prev, p_own, p_next = call(
        functools.partial(audio_partial, *dims),
        [sds(span, COLS + HD, f32)] * 3,
        (tile_list, tile_count) + group_keys + (az, rounds[1], rounds[groups - 1]),
        "audio_partial",
        flops=4 * 3 * span * GROUP * rows * COLS,
        smem=2,
    )
    r_next, r_prev = shift(p_prev, -GROUP), shift(p_next, GROUP)
    acc, marks = call(
        functools.partial(near_part, *dims),
        [sds(2 * rows, COLS, f32), sds(2 * rows, HD, f32)],
        (qa0, qa1) + group_keys + (az, *others),
        "near_part",
        flops=4 * 2 * rows * (GROUP * rows + tiles * aud) * COLS,
    )
    o2, o3, ao = call(
        functools.partial(far_part, *dims),
        [sds(padded, COLS), sds(padded, COLS), sds(2 * aud, COLS)],
        (q2, q3) + group_keys + (h0, h1, p_own, r_prev, r_next, az, *others),
        "far_part",
        flops=4 * 2 * rows * ((GROUP + 2) * rows + tiles * aud) * COLS,
    )
    o2, o3 = swap(o2, 2), swap(o3, 3)
    o0, o1 = call(
        functools.partial(last_part, *dims),
        [sds(padded, COLS)] * 2,
        (qa0, qa1, acc, marks, hk, hv2, hv3, ao),
        "last_part",
        flops=4 * 2 * rows * 2 * rows * COLS,
    )
    o1 = swap(o1, 1)
    video_out, audio_out = call(
        functools.partial(normalize, rows, aud),
        [sds(rows, H * HD), sds(aud, H * HD)],
        (video_gain[None], audio_gain[None], o0, o1, o2, o3),
        "normalize",
    )
    return (video_out, audio_out)


def solution(mesh):
    return jax.shard_map(
        on_device,
        mesh=mesh,
        in_specs=(
            P(("clips", "seq"), None),
            P(("clips", "seq"), None),
            P(("clips", "seq"), None),
            P(("clips", "seq"), None),
            P(("clips", "seq"), None),
            P(("clips", "seq"), None),
            P(("clips", "seq")),
            P("clips", None),
            P("clips"),
            P(),
            P(),
        ),
        out_specs=(P(("clips", "seq"), None), P(("clips", "seq"), None)),
        check_vma=False,
    )
```
